256 devices in a mesh: seq: 32 (over z, y), head: 8 (over x, core).
Axes of the slice: x: 4, y: 4, z: 8, core: 2. Of those that a mesh axis runs over, the one named last changes fastest.
Arguments:
- queries: bfloat16 [32768, 8192], P(('seq', 'head')), may hold values from -18 to 18
- keys: bfloat16 [32768, 1024], P(('seq', 'head')), may hold values from -6 to 6
- values: bfloat16 [32768, 1024], P(('seq', 'head')), may hold values from -6 to 6
- upstream: bfloat16 [32768, 8192], P(('seq', 'head')), may hold values from -96 to 96
- send_rows: int32 [32, 1536], P('seq'), may hold values from -1 to 1023, as said below
- recv_rows: int32 [32, 1024], P('seq'), may hold values from 0 to 1535, as said below
- doc_lengths: int32 [32, 4], P('seq'), may hold values from 1 to 512, 1024 in all within a row
- pair_docs: int32 [128], replicated, may hold values from 0 to 127, each once
- response_mask: int32 [32768], P('seq'), may hold values 0 or 1
- policy_logp: float32 [32768], P('seq'), may hold values from -2.5 to -0.05
- ref_logp: float32 [32768], P('seq'), may hold values from -2.5 to -0.05
Outputs:
- grad_queries: bfloat16 [32768, 8192], P(('seq', 'head'))
- key_row_gradient: bfloat16 [32768, 1024], P(('seq', 'head'))
- value_row_gradient: bfloat16 [32768, 1024], P(('seq', 'head'))
The draws below stay inside these ranges and needn't reach their ends.
Inputs may be any that keep to these rules, and one draw needn't show every extreme that they name: `send_rows`: entry o * 48 + k of loader group s names the row (of its 1024) that owner group o takes as its k-th row from s, or -1 for an empty slot. Every row of a loader group is named exactly once; in each block of 48 entries the named rows come first; every loader group fills some block completely. `recv_rows`: entry p of owner group o names the received slot s * 48 + k (k-th slot from loader group s) that holds its row p. The named slots of an owner group are distinct and are exactly the filled ones. `doc_lengths`: row o lists the lengths of owner group o's 4 dialogues in the order in which they fill its 1024 rows; each row sums to 1024. Dialogue j of owner group o has the number o * 4 + j. Pair k is the chosen dialogue pair_docs[2k] and the rejected dialogue pair_docs[2k+1]. `response_mask`: 1 marks a response token.
All inputs are finite; a program needn't handle non-finite values. No bound on the sum of `response_mask` on one device may be relied on, other than what follows from the above.
Results may differ from the reference program's by a relative error of at most 0.0088.
Values may be sent and summed in bfloat16 or wider, within the bound.
No kernel may reach another device: no remote copies, remote signals or barrier semaphores. Data moves between devices by JAX's collectives and lax.ppermute only.
A program may use at most 128 MiB of HBM per device.

```python
import math
import jax
import jax.numpy as jnp
import numpy as np
from jax import lax

QUERY_HEAD_COUNT = 64
KEY_VALUE_HEADS = 8
HEAD_SIZE = 128
DOC_OWN = 4
GROUP_TOKEN_ROWS = 1024
TOKEN_TOTAL = 32768
CAP = 48
DOCS = 128
N_SEQ = 32


def routing_tables(key):
    base = jax.random.fold_in(key, 7001)
    divided_keys = jax.random.split(base, 6)
    groups = TOKEN_TOTAL // GROUP_TOKEN_ROWS
    average = GROUP_TOKEN_ROWS // groups
    spread = average // 2
    capacity = average + spread
    halfway = groups // 2
    delta = jax.random.randint(divided_keys[0], (halfway,), -spread, spread + 1).astype(jnp.int32)
    delta = delta.at[0].set(spread)
    fills = jnp.concatenate([average + delta, average - delta]).astype(jnp.int32)
    fills = jax.random.permutation(divided_keys[1], fills)
    rotate_owner = jax.random.permutation(divided_keys[2], groups).astype(jnp.int32)
    rotate_loader = jax.random.permutation(divided_keys[3], groups).astype(jnp.int32)
    counts = fills[(rotate_owner[None, :] - rotate_loader[:, None]) % groups]
    loader_order = jax.vmap(lambda sub: jax.random.permutation(sub, groups))(jax.random.split(divided_keys[4], groups)).astype(jnp.int32)
    ordered = jnp.take_along_axis(counts, loader_order, axis=1)
    before = jnp.cumsum(ordered, axis=1) - ordered
    loader_index = jnp.arange(groups, dtype=jnp.int32)
    starts = jnp.zeros((groups, groups), jnp.int32).at[loader_index[:, None], loader_order].set(before)
    offset = jnp.arange(capacity, dtype=jnp.int32)
    send_table = jnp.where(offset[None, None, :] < counts[:, :, None], starts[:, :, None] + offset[None, None, :], -1)
    send_table = send_table.reshape(groups, groups * capacity).astype(jnp.int32)
    owner_order = jax.vmap(lambda sub: jax.random.permutation(sub, groups))(jax.random.split(divided_keys[5], groups)).astype(jnp.int32)
    run_length = jnp.take_along_axis(counts.T, owner_order, axis=1)
    run_end = jnp.cumsum(run_length, axis=1)
    position = jnp.arange(GROUP_TOKEN_ROWS, dtype=jnp.int32)
    which_run = jnp.sum((position[None, :, None] >= run_end[:, None, :]).astype(jnp.int32), axis=2)
    source = jnp.take_along_axis(owner_order, which_run, axis=1)
    run_start = jnp.take_along_axis(run_end - run_length, which_run, axis=1)
    recv_table = (source * capacity + position[None, :] - run_start).astype(jnp.int32)
    return (send_table, recv_table)


def draw_send_rows(key, part):
    return routing_tables(key)[0]


def draw_recv_rows(key, part):
    return routing_tables(key)[1]


def attention_inputs(key):
    base = jax.random.fold_in(key, 9103)
    divided_keys = jax.random.split(base, 3)
    rows_of_key = jnp.clip(jax.random.normal(divided_keys[0], (TOKEN_TOTAL, KEY_VALUE_HEADS * HEAD_SIZE), jnp.float32), -6.0, 6.0)
    query_rows = jnp.clip(jax.random.normal(divided_keys[2], (TOKEN_TOTAL, QUERY_HEAD_COUNT * HEAD_SIZE), jnp.float32), -6.0, 6.0)
    return (query_rows, rows_of_key)


def draw_queries(key, part):
    return attention_inputs(key)[0].astype(jnp.bfloat16)


def draw_keys(key, part):
    return attention_inputs(key)[1].astype(jnp.bfloat16)


def plant(values, stream_key, least, top_value):
    longest = values.shape.index(max(values.shape))
    spots = []
    for shift in (0, 1):
        where = [jax.random.randint(jax.random.fold_in(stream_key, axis), (), 0, length) for axis, length in enumerate(values.shape)]
        where[longest] = (where[longest] + shift) % values.shape[longest]
        spots.append(tuple(where))
    return values.at[spots[0]].set(least).at[spots[1]].set(top_value)


def levels(stream_key, shape, cuts, low, top_value):
    level, own = 1.0, jax.random.fold_in(stream_key, 6)
    for dim, parts in cuts:
        steps = jnp.exp(jax.random.uniform(jax.random.fold_in(own, dim), (parts,), jnp.float32, low / len(cuts), top_value / len(cuts)))
        level = level * jnp.repeat(steps, shape[dim] // parts).reshape([-1 if axis == dim else 1 for axis in range(len(shape))])
    return level


def profile(count, total, limit, slope):
    portions = [(1 << 20) // math.isqrt(rank ** slope) + 1 for rank in range(2, count + 1)]
    surplus, holding = total - limit - (count - 1), [1] * (count - 1)
    while surplus > 0:
        free = [i for i in range(count - 1) if holding[i] < limit]
        pool, left = sum([portions[i] for i in free]), surplus
        for i in free:
            addition = min(limit - holding[i], max(1, left * portions[i] // pool), surplus)
            holding[i] = holding[i] + addition
            surplus = surplus - addition
    return np.array([limit] + holding)


def uneven(own_key, count, total, reach, slope):
    if count == 2:
        one = jax.random.randint(own_key, (), max(1, total - reach), min(reach, total - 1) + 1)
        return jnp.stack([one, total - one])
    tallies = jnp.asarray(profile(count, total, reach, slope), jnp.int32)
    couples = (count - 1) // 2
    donor, sink = tallies[1:1 + 2 * couples:2], tallies[2:2 + 2 * couples:2]
    room = jnp.minimum(donor - 1, reach - sink)
    passed = jax.random.randint(jax.random.fold_in(own_key, 1), (couples,), 0, 1 << 20) % (room + 1)
    tallies = tallies.at[1:1 + 2 * couples:2].set(donor - passed).at[2:2 + 2 * couples:2].set(sink + passed)
    return tallies[jax.random.permutation(jax.random.fold_in(own_key, 2), count)]


def scatter_about(stream_key, extent, scale, reach, cuts=(), kind=jnp.bfloat16):
    entries = jax.random.normal(stream_key, extent, jnp.float32) * scale
    if len(cuts) > 0:
        entries = levels(stream_key, extent, cuts, -0.22, 0.18) * entries
    return jnp.clip(entries, min=-reach, max=reach).astype(kind)


def setup_inputs(seed: int = 0) -> dict:
    splits = jax.random.split(jax.random.key(seed), 12)
    return {
        "queries": draw_queries(jax.random.fold_in(splits[11], 71), 0),
        "keys": draw_keys(jax.random.fold_in(splits[11], 71), 0),
        "values": scatter_about(splits[2], (TOKEN_TOTAL, KEY_VALUE_HEADS * HEAD_SIZE), 1.0, 6.0, ((0, 256),)),
        "upstream": scatter_about(splits[3], (TOKEN_TOTAL, QUERY_HEAD_COUNT * HEAD_SIZE), 16.0, 96.0, ((0, 256),)),
        "send_rows": draw_send_rows(jax.random.fold_in(splits[11], 71), 0),
        "recv_rows": draw_recv_rows(jax.random.fold_in(splits[11], 71), 0),
        "doc_lengths": jax.vmap(lambda own: uneven(own, DOC_OWN, GROUP_TOKEN_ROWS, GROUP_TOKEN_ROWS // 2, 2))(jax.random.split(splits[6], N_SEQ)).reshape((N_SEQ, DOC_OWN)).astype(jnp.int32),
        "pair_docs": jax.random.permutation(splits[7], DOCS).astype(jnp.int32),
        "response_mask": plant((jax.random.randint(splits[8], (TOKEN_TOTAL,), 0, 4) < 3).astype(jnp.int32), jax.random.fold_in(splits[8], 1), 0, 1),
        "policy_logp": jnp.clip(-2.5 + 2.45 * jax.random.uniform(splits[9], (TOKEN_TOTAL,), jnp.float32) ** levels(splits[9], (TOKEN_TOTAL,), ((0, 32),), -0.2, 0.2), -2.5, -0.05),
        "ref_logp": jnp.clip(-2.5 + 2.45 * jax.random.uniform(splits[10], (TOKEN_TOTAL,), jnp.float32) ** levels(splits[10], (TOKEN_TOTAL,), ((0, 32),), -0.2, 0.2), -2.5, -0.05),
    }


dpo_beta = 0.1

def head_grads(query_block, key_block, value_block, grad_block, allowed, score_scale):
    scores = lax.dot_general(query_block, key_block, (((1,), (1,)), ((), ())), preferred_element_type=jnp.float32) * score_scale
    scores = jnp.where(allowed, scores, -1e+30)
    highest = lax.optimization_barrier(jnp.max(scores, axis=1, keepdims=True))
    lifted = jnp.exp(scores - highest)
    probs = lifted / lax.optimization_barrier(jnp.sum(lifted, axis=1, keepdims=True))
    probs_low = probs.astype(jnp.bfloat16)
    output = jnp.dot(probs_low, value_block, preferred_element_type=jnp.float32)
    row_dot = lax.optimization_barrier(jnp.sum(grad_block.astype(jnp.float32) * output, axis=1, keepdims=True))
    value_gradient = lax.dot_general(probs_low, grad_block, (((0,), (0,)), ((), ())), preferred_element_type=jnp.float32)
    grad_probs = lax.dot_general(grad_block, value_block, (((1,), (1,)), ((), ())), preferred_element_type=jnp.float32)
    grad_scores = (probs * (grad_probs - row_dot) * score_scale).astype(jnp.bfloat16)
    grad_query = jnp.dot(grad_scores, key_block, preferred_element_type=jnp.float32).astype(jnp.bfloat16)
    key_gradient = lax.dot_general(grad_scores, query_block, (((0,), (0,)), ((), ())), preferred_element_type=jnp.float32)
    return (grad_query, key_gradient, value_gradient)

def reference(queries, keys, values, upstream, send_rows, recv_rows, doc_lengths, pair_docs, response_mask, policy_logp, ref_logp):
    owners = jnp.arange(N_SEQ, dtype=jnp.int32)
    source = (recv_rows // CAP).astype(jnp.int32)
    within = (recv_rows % CAP).astype(jnp.int32)
    group_row = send_rows[source, owners[:, None] * CAP + within]
    loader_row = (source * GROUP_TOKEN_ROWS + group_row).astype(jnp.int32)
    position = jnp.arange(GROUP_TOKEN_ROWS, dtype=jnp.int32)
    doc_ends = jnp.cumsum(doc_lengths, axis=1).astype(jnp.int32)
    doc_of_row = lax.optimization_barrier(jnp.sum((position[None, :, None] >= doc_ends[:, None, :]).astype(jnp.int32), axis=2)).astype(jnp.int32)
    token_gap = (response_mask.astype(jnp.float32) * (policy_logp - ref_logp)).reshape(N_SEQ, GROUP_TOKEN_ROWS)
    member = doc_of_row[:, :, None] == jnp.arange(DOC_OWN, dtype=jnp.int32)[None, None, :]
    doc_gap = lax.optimization_barrier(jnp.sum(jnp.where(member, token_gap[:, :, None], 0.0), axis=1)).reshape(DOCS)
    chosen_docs = pair_docs[0::2]
    rejected_docs = pair_docs[1::2]
    margin = dpo_beta * (doc_gap[chosen_docs] - doc_gap[rejected_docs])
    pair_weight = dpo_beta * jax.nn.sigmoid(-margin)
    doc_coef = jnp.zeros((DOCS,), jnp.float32).at[chosen_docs].set(-pair_weight).at[rejected_docs].set(pair_weight)
    row_coef = jnp.take_along_axis(doc_coef.reshape(N_SEQ, DOC_OWN), doc_of_row, axis=1)
    group_share = QUERY_HEAD_COUNT // KEY_VALUE_HEADS
    score_scale = 1.0 / math.sqrt(HEAD_SIZE)

    def one_group(items):
        rows, coef_rows, docs = items
        query_rows = jnp.take(queries, rows, axis=0)
        rows_of_key = jnp.take(keys, rows, axis=0)
        rows_of_value = jnp.take(values, rows, axis=0)
        grad_out = (coef_rows[:, None] * jnp.take(upstream, rows, axis=0).astype(jnp.float32)).astype(jnp.bfloat16)
        allowed = (docs[:, None] == docs[None, :]) & (position[None, :] <= position[:, None])
        query_heads = query_rows.reshape(GROUP_TOKEN_ROWS, QUERY_HEAD_COUNT, HEAD_SIZE).transpose(1, 0, 2)
        grad_heads = grad_out.reshape(GROUP_TOKEN_ROWS, QUERY_HEAD_COUNT, HEAD_SIZE).transpose(1, 0, 2)
        heads_of_key = rows_of_key.reshape(GROUP_TOKEN_ROWS, KEY_VALUE_HEADS, HEAD_SIZE).transpose(1, 0, 2)
        heads_of_value = rows_of_value.reshape(GROUP_TOKEN_ROWS, KEY_VALUE_HEADS, HEAD_SIZE).transpose(1, 0, 2)

        def one_head(pieces):
            query_block, grad_block, head_index = pieces
            shared = head_index // group_share
            return head_grads(query_block, heads_of_key[shared], heads_of_value[shared], grad_block, allowed, score_scale)
        grad_query, key_gradient, value_gradient = lax.map(one_head, (query_heads, grad_heads, jnp.arange(QUERY_HEAD_COUNT, dtype=jnp.int32)))
        grad_query = grad_query.transpose(1, 0, 2).reshape(GROUP_TOKEN_ROWS, QUERY_HEAD_COUNT * HEAD_SIZE)
        key_gradient = key_gradient.reshape(KEY_VALUE_HEADS, group_share, GROUP_TOKEN_ROWS, HEAD_SIZE).sum(axis=1).astype(jnp.bfloat16)
        value_gradient = value_gradient.reshape(KEY_VALUE_HEADS, group_share, GROUP_TOKEN_ROWS, HEAD_SIZE).sum(axis=1).astype(jnp.bfloat16)
        key_gradient = key_gradient.transpose(1, 0, 2).reshape(GROUP_TOKEN_ROWS, KEY_VALUE_HEADS * HEAD_SIZE)
        value_gradient = value_gradient.transpose(1, 0, 2).reshape(GROUP_TOKEN_ROWS, KEY_VALUE_HEADS * HEAD_SIZE)
        return (grad_query, key_gradient, value_gradient)
    owner_query, key_at_owner, value_at_owner = lax.map(one_group, (loader_row, row_coef, doc_of_row))
    flattened_rows = loader_row.reshape(TOKEN_TOTAL)
    grad_queries = jnp.zeros((TOKEN_TOTAL, QUERY_HEAD_COUNT * HEAD_SIZE), jnp.bfloat16).at[flattened_rows].set(owner_query.reshape(TOKEN_TOTAL, QUERY_HEAD_COUNT * HEAD_SIZE))
    key_row_gradient = jnp.zeros((TOKEN_TOTAL, KEY_VALUE_HEADS * HEAD_SIZE), jnp.bfloat16).at[flattened_rows].set(key_at_owner.reshape(TOKEN_TOTAL, KEY_VALUE_HEADS * HEAD_SIZE))
    value_row_gradient = jnp.zeros((TOKEN_TOTAL, KEY_VALUE_HEADS * HEAD_SIZE), jnp.bfloat16).at[flattened_rows].set(value_at_owner.reshape(TOKEN_TOTAL, KEY_VALUE_HEADS * HEAD_SIZE))
    return (grad_queries, key_row_gradient, value_row_gradient)
```

```python
import math

import jax
import jax.numpy as jnp
from jax import lax
from jax.experimental import pallas as pl
from jax.experimental.pallas import tpu as pltpu
from jax.sharding import Mesh
from jax.sharding import PartitionSpec as P

D = 128
CAP = 48
KB = 128
NZ = 8
NY = 4
NH = 8
BETA = 0.1
BF = jnp.bfloat16
F32 = jnp.float32


def dot(a, b, ca, cb):
    return lax.dot_general(a, b, (((ca,), (cb,)), ((), ())), preferred_element_type=F32)


def attention_kernel(
    rng, q_ref, u_ref, kv_ref, p_ref, st_ref, c_ref, gq_ref, gkv_ref, s_scr, dp_scr, kt_scr, dq_acc, gk_acc, gv_acc
):
    owner = pl.program_id(0)
    heads = q_ref.shape[3] // D
    lanes = heads * CAP
    scale = 1.0 / math.sqrt(D)
    kt_scr[...] = kv_ref[0, :, :D].astype(F32).T.astype(BF)
    gk_acc[...] = jnp.zeros_like(gk_acc)
    gv_acc[...] = jnp.zeros_like(gv_acc)

    def stack(block):
        return jnp.concatenate([block[:, h * D : (h + 1) * D] for h in range(heads)], axis=0)

    def fold(x, op):
        return op(x.reshape(KB // 8, 8, lanes), axis=0)

    for y in range(NY):
        q = stack(q_ref[y, 0])
        coef = c_ref[0, y * CAP : (y + 1) * CAP, :]
        g = stack((u_ref[y, 0].astype(F32) * coef).astype(BF))
        pos = p_ref[0, y : y + 1, :]
        start = st_ref[0, y : y + 1, :]
        lo = rng[0, owner * NY + y]
        hi = rng[1, owner * NY + y]

        def score_pass(j, top):
            ks = pl.multiple_of(j * KB, KB)
            s = dot(kv_ref[0, pl.ds(ks, KB), :D], q, 1, 1) * scale
            key = lax.broadcasted_iota(jnp.int32, (KB, lanes), 0) + ks
            s = jnp.where((key >= start) & (key <= pos), s, -1e30)
            s_scr[pl.ds(ks, KB), :] = s
            return jnp.maximum(top, fold(s, jnp.max))

        top = lax.fori_loop(lo, hi, score_pass, jnp.full((8, lanes), -1e30, F32))
        top = jnp.max(top, axis=0, keepdims=True)

        def weigh_pass(j, sums):
            total, cross = sums
            ks = pl.multiple_of(j * KB, KB)
            e = jnp.exp(s_scr[pl.ds(ks, KB), :] - top)
            dp = dot(kv_ref[0, pl.ds(ks, KB), D:], g, 1, 1)
            s_scr[pl.ds(ks, KB), :] = e
            dp_scr[pl.ds(ks, KB), :] = dp
            return (total + fold(e, jnp.sum), cross + fold(e * dp, jnp.sum))

        zero = jnp.zeros((8, lanes), F32)
        total, cross = lax.fori_loop(lo, hi, weigh_pass, (zero, zero))
        inverse = 1.0 / jnp.sum(total, axis=0, keepdims=True)
        row_dot = jnp.sum(cross, axis=0, keepdims=True) * inverse
        dq_acc[...] = jnp.zeros_like(dq_acc)

        def grad_pass(j, carry):
            ks = pl.multiple_of(j * KB, KB)
            probs = s_scr[pl.ds(ks, KB), :] * inverse
            gs = (probs * (dp_scr[pl.ds(ks, KB), :] - row_dot) * scale).astype(BF)
            gv_acc[pl.ds(ks, KB), :] += dot(probs.astype(BF), g, 1, 0)
            gk_acc[pl.ds(ks, KB), :] += dot(gs, q, 1, 0)
            dq_acc[...] += dot(kt_scr[:, pl.ds(ks, KB)], gs, 1, 0)
            return carry

        lax.fori_loop(lo, hi, grad_pass, 0)
        gq = dq_acc[...].T.astype(BF)
        for h in range(heads):
            gq_ref[y, 0, :, h * D : (h + 1) * D] = gq[h * CAP : (h + 1) * CAP, :]
    gkv_ref[0, :, :D] = gk_acc[...].astype(BF)
    gkv_ref[0, :, D:] = gv_acc[...].astype(BF)


def attention(rng, q, u, kv, pos, start, coef):
    rows = kv.shape[1]
    width = q.shape[3]
    lanes = (width // D) * CAP
    slot = pl.BlockSpec((NY, 1, CAP, width), lambda i, r: (0, i, 0, 0))
    pair = pl.BlockSpec((1, rows, 2 * D), lambda i, r: (i, 0, 0))
    lane = pl.BlockSpec((1, NY, lanes), lambda i, r: (i, 0, 0))
    return pl.pallas_call(
        attention_kernel,
        grid_spec=pltpu.PrefetchScalarGridSpec(
            num_scalar_prefetch=1,
            grid=(NZ,),
            in_specs=[slot, slot, pair, lane, lane, pl.BlockSpec((1, NY * CAP, 1), lambda i, r: (i, 0, 0))],
            out_specs=[slot, pair],
            scratch_shapes=[
                pltpu.VMEM((rows, lanes), F32),
                pltpu.VMEM((rows, lanes), F32),
                pltpu.VMEM((D, rows), BF),
                pltpu.VMEM((D, lanes), F32),
                pltpu.VMEM((rows, D), F32),
                pltpu.VMEM((rows, D), F32),
            ],
        ),
        out_shape=[jax.ShapeDtypeStruct(q.shape, BF), jax.ShapeDtypeStruct(kv.shape, BF)],
        name="owner_attention",
    )(rng, q, u, kv, pos, start, coef)


def pick(index, count, rows):
    hot = index[:, None] == jnp.arange(count, dtype=jnp.int32)[None, :]
    return dot(hot.astype(BF), rows, 1, 0).astype(BF)


def place(index, count, rows):
    hot = jnp.arange(count, dtype=jnp.int32)[:, None] == index[None, :]
    return dot(hot.astype(BF), rows, 1, 0).astype(BF)


def body(
    queries, keys, values, upstream, send_rows, recv_rows, doc_lengths, pair_docs, response_mask, policy_logp, ref_logp
):
    tok = queries.shape[0]
    rows = tok * NH
    width = queries.shape[1] // NH
    seq = ("z", "y")
    slots = send_rows.shape[1]
    my_y = lax.axis_index("y")
    send = send_rows[0]
    send_y = send.reshape(NZ, NY, CAP).transpose(1, 0, 2).reshape(slots)
    recv = recv_rows[0]

    with jax.named_scope("kv_in"):
        kv = jnp.concatenate([keys.reshape(tok, NH, D), values.reshape(tok, NH, D)], axis=2).transpose(1, 0, 2)
        kv = lax.all_to_all(kv, "head", 0, 0).reshape(rows, 2 * D)
        kv = pick(send, rows, kv).reshape(NZ * NY, CAP, 2 * D)
        kv = lax.all_to_all(kv, seq, 0, 0).reshape(slots, 2 * D)
        kv = pick(recv, slots, kv)
        kv = lax.all_gather(kv, "z", axis=0)

    with jax.named_scope("meta"):
        place_of = jnp.arange(rows, dtype=jnp.int32)
        slot_id = jnp.arange(slots, dtype=jnp.int32)
        pos = jnp.sum(jnp.where(recv[None, :] == slot_id[:, None], place_of[None, :] + 1, 0), axis=1) - 1
        ends = jnp.cumsum(doc_lengths[0])
        doc_row = jnp.sum((place_of[:, None] >= ends[None, :]).astype(jnp.int32), axis=1)
        member = doc_row[:, None] == jnp.arange(4, dtype=jnp.int32)[None, :]
        gap_row = response_mask.astype(F32) * (policy_logp - ref_logp)
        gap = jnp.sum(jnp.where(member, gap_row[:, None], 0.0), axis=0)
        part = jnp.broadcast_to(pos.astype(F32).reshape(NZ, 1, NY * CAP), (NZ, NY, NY * CAP)).reshape(NZ * NY, NY * CAP)
        small = jnp.broadcast_to(
            jnp.concatenate([gap, ends.astype(F32), jnp.zeros((56,), F32)])[None, :], (NZ * NY, 64)
        )
        got = lax.all_to_all(jnp.concatenate([part, small], axis=1), seq, 0, 0)
        gaps = got[:, 192:196].reshape(128)
        mine = lax.dynamic_index_in_dim(got.reshape(NZ, NY, 256), my_y, 1, keepdims=False)
        other = pair_docs.reshape(64, 2)[:, ::-1].reshape(128)
        doc_id = jnp.arange(128, dtype=jnp.int32)
        own_hot = pair_docs[:, None] == doc_id[None, :]
        sign = 1.0 - 2.0 * (doc_id % 2).astype(F32)
        own_gap = jnp.sum(jnp.where(own_hot, gaps[None, :], 0.0), axis=1)
        other_gap = jnp.sum(jnp.where(other[:, None] == doc_id[None, :], gaps[None, :], 0.0), axis=1)
        margin = BETA * (own_gap - other_gap) * sign
        weight = -sign * (BETA * jax.nn.sigmoid(-margin))
        doc_coef = jnp.sum(jnp.where(own_hot, weight[:, None], 0.0), axis=0)
        my_coef = lax.dynamic_index_in_dim(doc_coef.reshape(NZ, NY, 4), my_y, 1, keepdims=False)
        q_pos = mine[:, :192].astype(jnp.int32)
        q_ends = mine[:, 196:200].astype(jnp.int32)
        past = q_pos[:, :, None] >= q_ends[:, None, :]
        q_doc = jnp.sum(past.astype(jnp.int32), axis=2)
        q_start = jnp.max(jnp.where(past, q_ends[:, None, :], 0), axis=2)
        in_doc = (q_doc[:, :, None] == jnp.arange(4, dtype=jnp.int32)) & (q_pos[:, :, None] >= 0)
        coef = jnp.sum(jnp.where(in_doc, my_coef[:, None, :], 0.0), axis=2)
        q_pos = q_pos.reshape(NZ, NY, CAP)
        q_start = q_start.reshape(NZ, NY, CAP)
        last = jnp.max(q_pos, axis=2) // KB + 1
        first = jnp.min(jnp.where(q_pos >= 0, q_start, rows), axis=2) // KB
        last = jnp.clip(last, 0, rows // KB)
        first = jnp.clip(first, 0, last)
        rng = jnp.stack([first.reshape(-1), last.reshape(-1)])
        heads = width // D
        pos_lane = jnp.tile(q_pos, (1, 1, heads))
        start_lane = jnp.tile(q_start, (1, 1, heads))

    def move_in(x):
        x = x.reshape(tok, NH, width).transpose(1, 0, 2)
        x = lax.all_to_all(x, "head", 0, 0).reshape(rows, width)
        x = pick(send_y, rows, x).reshape(NY, slots // NY, width)
        return lax.all_to_all(x, "y", 0, 0).reshape(NY, NZ, CAP, width)

    with jax.named_scope("q_in"):
        q = move_in(queries)
    with jax.named_scope("u_in"):
        u = move_in(upstream)

    gq, gkv = attention(rng, q, u, kv, pos_lane, start_lane, coef[:, :, None])

    with jax.named_scope("kv_out"):
        gkv = lax.psum_scatter(gkv, "z", scatter_dimension=0)
        gkv = pick(pos, rows, gkv).reshape(NZ * NY, CAP, 2 * D)
        gkv = lax.all_to_all(gkv, seq, 0, 0).reshape(slots, 2 * D)
        gkv = place(send, rows, gkv).reshape(NH, tok, 2 * D)
        gkv = lax.all_to_all(gkv, "head", 0, 0).transpose(1, 0, 2)
        gk = gkv[:, :, :D].reshape(tok, NH * D)
        gv = gkv[:, :, D:].reshape(tok, NH * D)
    with jax.named_scope("q_out"):
        gq = lax.all_to_all(gq.reshape(NY, slots // NY, width), "y", 0, 0).reshape(slots, width)
        gq = place(send_y, rows, gq).reshape(NH, tok, width)
        gq = lax.all_to_all(gq, "head", 0, 0).transpose(1, 0, 2).reshape(tok, NH * width)
    return (gq, gk, gv)


def solution(mesh):
    grid = Mesh(mesh.devices.reshape(NZ, NY, NH), ("z", "y", "head"))
    tokens = P(("z", "y", "head"), None)
    group = P(("z", "y"), None)
    line = P(("z", "y"))
    return jax.shard_map(
        body,
        mesh=grid,
        in_specs=(tokens, tokens, tokens, tokens, group, group, group, P(), line, line, line),
        out_specs=(tokens, tokens, tokens),
        check_vma=False,
    )
```

```python
import math

import jax
import jax.numpy as jnp
from jax import lax
from jax.experimental import pallas as pl
from jax.experimental.pallas import tpu as pltpu
from jax.sharding import Mesh
from jax.sharding import PartitionSpec as P


D = 128
CAP = 48
NZ = 8
NY = 4
NH = 8
BETA = 0.1
BF = jnp.bfloat16
F32 = jnp.float32


def dot(a, b, ca, cb):
    return lax.dot_general(a, b, (((ca,), (cb,)), ((), ())), preferred_element_type=F32)


WINDOWS = (1, 2, 3, 4, 5, 8)


def attention_kernel(rng, *refs):
    q_in, u_in = refs[:NY], refs[NY : 2 * NY]
    kv_ref, p_ref, st_ref, c_ref = refs[2 * NY : 2 * NY + 4]
    gq_out, gkv_ref = refs[2 * NY + 4 : 3 * NY + 4], refs[3 * NY + 4]
    q_scr, u_scr, gq_scr, gk_acc, gv_acc = refs[3 * NY + 5 :]
    owner = pl.program_id(0)
    heads = q_scr.shape[2] // D
    lanes = heads * CAP
    scale = 1.0 / math.sqrt(D)
    gk_acc[...] = jnp.zeros_like(gk_acc)
    gv_acc[...] = jnp.zeros_like(gv_acc)
    for y in range(NY):
        q_scr[y] = q_in[y][0]
        u_scr[y] = u_in[y][0]

    def stack(block):
        return jnp.concatenate([block[:, h * D : (h + 1) * D] for h in range(heads)], axis=0)

    def window(y, base, size):
        q = stack(q_scr[y])
        g = stack((u_scr[y].astype(F32) * c_ref[0, y]).astype(BF))
        pos = p_ref[0, y]
        start = st_ref[0, y]
        keys = kv_ref[0, pl.ds(base, size), :D]
        vals = kv_ref[0, pl.ds(base, size), D:]
        s = dot(keys, q, 1, 1) * scale
        key = lax.broadcasted_iota(jnp.int32, (size, lanes), 0) + base
        s = jnp.where((key >= start) & (key <= pos), s, -1e30)
        e = jnp.exp(s - jnp.max(s, axis=0, keepdims=True))
        dp = dot(vals, g, 1, 1)
        inverse = 1.0 / jnp.sum(e, axis=0, keepdims=True)
        row_dot = jnp.sum(e * dp, axis=0, keepdims=True) * inverse
        probs = e * inverse
        gs = (probs * (dp - row_dot) * scale).astype(BF)
        gv_acc[pl.ds(base, size), :] += dot(probs.astype(BF), g, 1, 0)
        gk_acc[pl.ds(base, size), :] += dot(gs, q, 1, 0)
        gq = dot(keys.T, gs, 1, 0).T.astype(BF)
        for h in range(heads):
            gq_scr[y, :, h * D : (h + 1) * D] = gq[h * CAP : (h + 1) * CAP, :]

    def one(y, carry):
        base = pl.multiple_of(rng[0, owner * NY + y], 16)
        blocks = rng[1, owner * NY + y]
        for n in WINDOWS:
            pl.when(blocks == n)(lambda n=n: window(y, base, n * 128))
        return carry

    lax.fori_loop(0, NY, one, 0)
    for y in range(NY):
        gq_out[y][0] = gq_scr[y]
    gkv_ref[0, :, :D] = gk_acc[...].astype(BF)
    gkv_ref[0, :, D:] = gv_acc[...].astype(BF)


def attention(rng, q, u, kv, pos, start, coef):
    rows = kv.shape[1]
    width = q[0].shape[2]
    lanes = (width // D) * CAP
    slot = pl.BlockSpec((1, CAP, width), lambda i, r: (i, 0, 0))
    pair = pl.BlockSpec((1, rows, 2 * D), lambda i, r: (i, 0, 0))
    lane = pl.BlockSpec((1, NY, 1, lanes), lambda i, r: (i, 0, 0, 0))
    out = pl.pallas_call(
        attention_kernel,
        grid_spec=pltpu.PrefetchScalarGridSpec(
            num_scalar_prefetch=1,
            grid=(NZ,),
            in_specs=[slot] * (2 * NY) + [pair, lane, lane, pl.BlockSpec((1, NY, CAP, 1), lambda i, r: (i, 0, 0, 0))],
            out_specs=[slot] * NY + [pair],
            scratch_shapes=[pltpu.VMEM((NY, CAP, width), BF)] * 3 + [pltpu.VMEM((rows, D), F32)] * 2,
        ),
        out_shape=[jax.ShapeDtypeStruct(q[0].shape, BF)] * NY + [jax.ShapeDtypeStruct(kv.shape, BF)],
        name="owner_attention",
    )(rng, *q, *u, kv, pos, start, coef)
    return out[:NY], out[NY]


def split_kernel(me_ref, *refs):
    count = len(refs) - NH
    ins, outs = refs[:count], refs[count:]
    width = ins[0].shape[1] // NH
    for j in range(NH):
        to = lax.rem(me_ref[0] + j, NH)
        cols = pl.ds(pl.multiple_of(to * width, 128), width)
        for k in range(count):
            outs[j][:, k * width : (k + 1) * width] = ins[k][:, cols]


def split(me, arrays):
    tok = arrays[0].shape[0]
    width = arrays[0].shape[1] // NH * len(arrays)
    return pl.pallas_call(
        split_kernel,
        in_specs=[pl.BlockSpec(memory_space=pltpu.SMEM)] + [pl.BlockSpec(memory_space=pltpu.VMEM)] * len(arrays),
        out_specs=[pl.BlockSpec(memory_space=pltpu.VMEM)] * NH,
        out_shape=[jax.ShapeDtypeStruct((tok, width), BF)] * NH,
        name="split_heads",
    )(me, *arrays)


def join_kernel(me_ref, *refs):
    ins, outs = refs[:NH], refs[NH:]
    width = outs[0].shape[1] // NH
    for j in range(NH):
        src = lax.rem(me_ref[0] + (NH - j), NH)
        cols = pl.ds(pl.multiple_of(src * width, 128), width)
        for k in range(len(outs)):
            outs[k][:, cols] = ins[j][:, k * width : (k + 1) * width]


def join(me, pieces, count):
    tok, width = pieces[0].shape
    return pl.pallas_call(
        join_kernel,
        in_specs=[pl.BlockSpec(memory_space=pltpu.SMEM)] + [pl.BlockSpec(memory_space=pltpu.VMEM)] * NH,
        out_specs=[pl.BlockSpec(memory_space=pltpu.VMEM)] * count,
        out_shape=[jax.ShapeDtypeStruct((tok, width // count * NH), BF)] * count,
        name="join_heads",
    )(me, *pieces)


def swap_heads(pieces):
    return [pieces[0]] + [
        lax.ppermute(pieces[j], "head", [(h, (h + j) % NH) for h in range(NH)]) for j in range(1, NH)
    ]


def swap_owners(pieces, sign):
    return [pieces[0]] + [
        lax.ppermute(pieces[j], "y", [(h, (h + sign * j) % NY) for h in range(NY)]) for j in range(1, NY)
    ]


def pack_kernel(idx_ref, *refs):
    pieces, outs = refs[:NH], refs[NH:]
    block = jnp.concatenate([p[...] for p in pieces], axis=0)
    step = outs[0].shape[0]
    for j, out in enumerate(outs):
        idx = idx_ref[j * step : (j + 1) * step, :]
        hot = idx == lax.broadcasted_iota(jnp.int32, (step, block.shape[0]), 1)
        out[...] = dot(hot.astype(F32).astype(BF), block, 1, 0).astype(BF)


def pack(idx, pieces, count):
    return pl.pallas_call(
        pack_kernel,
        out_shape=[jax.ShapeDtypeStruct((idx.shape[0] // count, pieces[0].shape[1]), BF)] * count,
        name="pack_rows",
    )(idx, *pieces)


def unpack_kernel(idx_ref, *refs):
    ins, outs = refs[: len(refs) - NH], refs[len(refs) - NH :]
    tok = outs[0].shape[0]
    block = jnp.concatenate([p[...] for p in ins], axis=0)
    for j in range(NH):
        row = lax.broadcasted_iota(jnp.int32, (tok, block.shape[0]), 0) + j * tok
        hot = (row == idx_ref[...]).astype(F32).astype(BF)
        outs[j][...] = dot(hot, block, 1, 0).astype(BF)


def unpack(idx, pieces, tok):
    return pl.pallas_call(
        unpack_kernel,
        out_shape=[jax.ShapeDtypeStruct((tok, pieces[0].shape[1]), BF)] * NH,
        name="unpack_rows",
    )(idx, *pieces)


def pick(index, count, rows):
    hot = index[:, None] == jnp.arange(count, dtype=jnp.int32)[None, :]
    return dot(hot.astype(BF), rows, 1, 0).astype(BF)


def body(
    queries, keys, values, upstream, send_rows, recv_rows, doc_lengths, pair_docs, response_mask, policy_logp, ref_logp
):
    tok = queries.shape[0]
    rows = tok * NH
    width = queries.shape[1] // NH
    seq = ("z", "y")
    slots = send_rows.shape[1]
    my_y = lax.axis_index("y")
    send = send_rows[0]
    ahead = (my_y + jnp.arange(NY, dtype=jnp.int32)) % NY
    behind = (my_y - jnp.arange(NY, dtype=jnp.int32)) % NY
    send_y = jnp.take(send.reshape(NZ, NY, CAP), ahead, axis=1).transpose(1, 0, 2).reshape(slots)
    recv = recv_rows[0]
    me = lax.axis_index("head")
    me_arr = me.reshape(1).astype(jnp.int32)

    def turned(index, sign):
        piece = (sign * (index // tok - me)) % NH
        return jnp.where(index >= 0, piece * tok + index % tok, -1)

    kv = split(me_arr, [keys, values])
    kv = swap_heads(kv)
    (kv,) = pack(turned(send, -1)[:, None], kv, 1)
    kv = lax.all_to_all(kv.reshape(NZ * NY, CAP, 2 * D), seq, 0, 0).reshape(slots, 2 * D)
    kv = pick(recv, slots, kv)
    kv = lax.all_gather(kv, "z", axis=0)

    place_of = jnp.arange(rows, dtype=jnp.int32)
    slot_id = jnp.arange(slots, dtype=jnp.int32)
    pos = jnp.sum(jnp.where(recv[None, :] == slot_id[:, None], place_of[None, :] + 1, 0), axis=1) - 1
    ends = jnp.cumsum(doc_lengths[0])
    doc_row = jnp.sum((place_of[:, None] >= ends[None, :]).astype(jnp.int32), axis=1)
    member = doc_row[:, None] == jnp.arange(4, dtype=jnp.int32)[None, :]
    gap_row = response_mask.astype(F32) * (policy_logp - ref_logp)
    gap = jnp.sum(jnp.where(member, gap_row[:, None], 0.0), axis=0)
    part = jnp.broadcast_to(pos.astype(F32).reshape(NZ, 1, NY * CAP), (NZ, NY, NY * CAP)).reshape(NZ * NY, NY * CAP)
    small = jnp.broadcast_to(jnp.concatenate([gap, ends.astype(F32), jnp.zeros((56,), F32)])[None, :], (NZ * NY, 64))
    got = lax.all_to_all(jnp.concatenate([part, small], axis=1), seq, 0, 0)
    gaps = got[:, 192:196].reshape(128)
    mine = lax.dynamic_index_in_dim(got.reshape(NZ, NY, 256), my_y, 1, keepdims=False)
    other = pair_docs.reshape(64, 2)[:, ::-1].reshape(128)
    doc_id = jnp.arange(128, dtype=jnp.int32)
    own_hot = pair_docs[:, None] == doc_id[None, :]
    sign = 1.0 - 2.0 * (doc_id % 2).astype(F32)
    own_gap = jnp.sum(jnp.where(own_hot, gaps[None, :], 0.0), axis=1)
    other_gap = jnp.sum(jnp.where(other[:, None] == doc_id[None, :], gaps[None, :], 0.0), axis=1)
    margin = BETA * (own_gap - other_gap) * sign
    weight = -sign * (BETA * jax.nn.sigmoid(-margin))
    doc_coef = jnp.sum(jnp.where(own_hot, weight[:, None], 0.0), axis=0)
    my_coef = lax.dynamic_index_in_dim(doc_coef.reshape(NZ, NY, 4), my_y, 1, keepdims=False)
    q_pos = mine[:, :192].astype(jnp.int32)
    q_ends = mine[:, 196:200].astype(jnp.int32)
    past = q_pos[:, :, None] >= q_ends[:, None, :]
    q_doc = jnp.sum(past.astype(jnp.int32), axis=2)
    q_start = jnp.max(jnp.where(past, q_ends[:, None, :], 0), axis=2)
    in_doc = (q_doc[:, :, None] == jnp.arange(4, dtype=jnp.int32)) & (q_pos[:, :, None] >= 0)
    coef = jnp.sum(jnp.where(in_doc, my_coef[:, None, :], 0.0), axis=2)
    q_pos = jnp.take(q_pos.reshape(NZ, NY, CAP), behind, axis=1)
    q_start = jnp.take(q_start.reshape(NZ, NY, CAP), behind, axis=1)
    coef = jnp.take(coef.reshape(NZ, NY, CAP), behind, axis=1)[:, :, :, None]
    past_last = jnp.max(q_pos, axis=2) + 1
    first = jnp.min(jnp.where(q_pos >= 0, q_start, rows), axis=2)
    first = jnp.clip(jnp.minimum(first, past_last) // 16 * 16, 0, rows - 128)
    blocks = jnp.clip((past_last - first + 127) // 128, 1, 8)
    blocks = jnp.where(blocks > 5, 8, blocks)
    first = jnp.minimum(first, rows - 128 * blocks)
    rng = jnp.stack([first.reshape(-1), blocks.reshape(-1)])
    heads = width // D
    pos_lane = jnp.tile(q_pos, (1, 1, heads))[:, :, None, :]
    start_lane = jnp.tile(q_start, (1, 1, heads))[:, :, None, :]

    in_index = turned(send_y, -1)[:, None]
    out_index = turned(send_y, 1)[None, :]

    def move_in(x):
        x = split(me_arr, [x])
        x = swap_heads(x)
        x = pack(in_index, x, NY)
        x = swap_owners(x, 1)
        return [t.reshape(NZ, CAP, width) for t in x]

    q = move_in(queries)
    u = move_in(upstream)

    gq, gkv = attention(rng, q, u, kv, pos_lane, start_lane, coef)

    gkv = lax.psum_scatter(gkv, "z", scatter_dimension=0)
    gkv = pick(pos, rows, gkv).reshape(NZ * NY, CAP, 2 * D)
    gkv = lax.all_to_all(gkv, seq, 0, 0).reshape(slots, 2 * D)
    gkv = unpack(turned(send, 1)[None, :], [gkv], tok)
    gkv = swap_heads(gkv)
    gk, gv = join(me_arr, gkv, 2)
    gq = swap_owners([t.reshape(NZ * CAP, width) for t in gq], -1)
    gq = unpack(out_index, gq, tok)
    gq = swap_heads(gq)
    (gq,) = join(me_arr, gq, 1)
    return (gq, gk, gv)


def solution(mesh):
    grid = Mesh(mesh.devices.reshape(NZ, NY, NH), ("z", "y", "head"))
    tokens = P(("z", "y", "head"), None)
    group = P(("z", "y"), None)
    line = P(("z", "y"))
    return jax.shard_map(
        body,
        mesh=grid,
        in_specs=(tokens, tokens, tokens, tokens, group, group, group, P(), line, line, line),
        out_specs=(tokens, tokens, tokens),
        check_vma=False,
    )
```

```python
import math

import jax
import jax.numpy as jnp
from jax import lax
from jax.experimental import pallas as pl
from jax.experimental.pallas import tpu as pltpu
from jax.sharding import Mesh
from jax.sharding import PartitionSpec as P


D = 128
CAP = 48
NZ = 8
NY = 4
NH = 8
BETA = 0.1
BF = jnp.bfloat16
F32 = jnp.float32


def dot(a, b, ca, cb):
    return lax.dot_general(a, b, (((ca,), (cb,)), ((), ())), preferred_element_type=F32)


WINDOWS = (1, 2, 3, 4, 5, 8)


def attention_kernel(rng, *refs):
    q_in, u_in = refs[:NY], refs[NY : 2 * NY]
    kv_ref, p_ref, st_ref, c_ref = refs[2 * NY : 2 * NY + 4]
    gq_out, gkv_ref = refs[2 * NY + 4 : 3 * NY + 4], refs[3 * NY + 4]
    q_scr, u_scr, gq_scr, gk_acc, gv_acc = refs[3 * NY + 5 :]
    owner = pl.program_id(0)
    heads = q_scr.shape[2] // D
    lanes = heads * CAP
    scale = 1.0 / math.sqrt(D)
    gk_acc[...] = jnp.zeros_like(gk_acc)
    gv_acc[...] = jnp.zeros_like(gv_acc)
    for y in range(NY):
        q_scr[y] = q_in[y][0]
        u_scr[y] = u_in[y][0]

    def stack(block):
        return jnp.concatenate([block[:, h * D : (h + 1) * D] for h in range(heads)], axis=0)

    def window(y, base, size):
        q = stack(q_scr[y])
        g = stack((u_scr[y].astype(F32) * c_ref[0, y]).astype(BF))
        pos = p_ref[0, y]
        start = st_ref[0, y]
        keys = kv_ref[0, pl.ds(base, size), :D]
        vals = kv_ref[0, pl.ds(base, size), D:]
        s = dot(keys, q, 1, 1) * scale
        key = lax.broadcasted_iota(jnp.int32, (size, lanes), 0) + base
        s = jnp.where((key >= start) & (key <= pos), s, -1e30)
        e = jnp.exp(s - jnp.max(s, axis=0, keepdims=True))
        dp = dot(vals, g, 1, 1)
        inverse = 1.0 / jnp.sum(e, axis=0, keepdims=True)
        row_dot = jnp.sum(e * dp, axis=0, keepdims=True) * inverse
        probs = e * inverse
        gs = (probs * (dp - row_dot) * scale).astype(BF)
        gv_acc[pl.ds(base, size), :] += dot(probs.astype(BF), g, 1, 0)
        gk_acc[pl.ds(base, size), :] += dot(gs, q, 1, 0)
        gq = dot(keys.T, gs, 1, 0).T.astype(BF)
        for h in range(heads):
            gq_scr[y, :, h * D : (h + 1) * D] = gq[h * CAP : (h + 1) * CAP, :]

    def one(y, carry):
        base = pl.multiple_of(rng[0, owner * NY + y], 16)
        blocks = rng[1, owner * NY + y]
        for n in WINDOWS:
            pl.when(blocks == n)(lambda n=n: window(y, base, n * 128))
        return carry

    lax.fori_loop(0, NY, one, 0)
    for y in range(NY):
        gq_out[y][0] = gq_scr[y]
    gkv_ref[0, :, :D] = gk_acc[...].astype(BF)
    gkv_ref[0, :, D:] = gv_acc[...].astype(BF)


def attention(rng, q, u, kv, pos, start, coef):
    rows = kv.shape[1]
    width = q[0].shape[2]
    lanes = (width // D) * CAP
    slot = pl.BlockSpec((1, CAP, width), lambda i, r: (i, 0, 0))
    pair = pl.BlockSpec((1, rows, 2 * D), lambda i, r: (i, 0, 0))
    lane = pl.BlockSpec((1, NY, 1, lanes), lambda i, r: (i, 0, 0, 0))
    out = pl.pallas_call(
        attention_kernel,
        grid_spec=pltpu.PrefetchScalarGridSpec(
            num_scalar_prefetch=1,
            grid=(NZ,),
            in_specs=[slot] * (2 * NY) + [pair, lane, lane, pl.BlockSpec((1, NY, CAP, 1), lambda i, r: (i, 0, 0, 0))],
            out_specs=[slot] * NY + [pair],
            scratch_shapes=[pltpu.VMEM((NY, CAP, width), BF)] * 3 + [pltpu.VMEM((rows, D), F32)] * 2,
        ),
        out_shape=[jax.ShapeDtypeStruct(q[0].shape, BF)] * NY + [jax.ShapeDtypeStruct(kv.shape, BF)],
        name="owner_attention",
    )(rng, *q, *u, kv, pos, start, coef)
    return out[:NY], out[NY]


def split_kernel(me_ref, *refs):
    count = len(refs) - NH
    ins, outs = refs[:count], refs[count:]
    width = ins[0].shape[1] // NH
    for j in range(NH):
        to = lax.rem(me_ref[0] + j, NH)
        cols = pl.ds(pl.multiple_of(to * width, 128), width)
        for k in range(count):
            outs[j][:, k * width : (k + 1) * width] = ins[k][:, cols]


def split(me, arrays):
    tok = arrays[0].shape[0]
    width = arrays[0].shape[1] // NH * len(arrays)
    return pl.pallas_call(
        split_kernel,
        in_specs=[pl.BlockSpec(memory_space=pltpu.SMEM)] + [pl.BlockSpec(memory_space=pltpu.VMEM)] * len(arrays),
        out_specs=[pl.BlockSpec(memory_space=pltpu.VMEM)] * NH,
        out_shape=[jax.ShapeDtypeStruct((tok, width), BF)] * NH,
        name="split_heads",
    )(me, *arrays)


def join_kernel(me_ref, *refs):
    ins, outs = refs[:NH], refs[NH:]
    width = outs[0].shape[1] // NH
    for j in range(NH):
        src = lax.rem(me_ref[0] + (NH - j), NH)
        cols = pl.ds(pl.multiple_of(src * width, 128), width)
        for k in range(len(outs)):
            outs[k][:, cols] = ins[j][:, k * width : (k + 1) * width]


def join(me, pieces, count):
    tok, width = pieces[0].shape
    return pl.pallas_call(
        join_kernel,
        in_specs=[pl.BlockSpec(memory_space=pltpu.SMEM)] + [pl.BlockSpec(memory_space=pltpu.VMEM)] * NH,
        out_specs=[pl.BlockSpec(memory_space=pltpu.VMEM)] * count,
        out_shape=[jax.ShapeDtypeStruct((tok, width // count * NH), BF)] * count,
        name="join_heads",
    )(me, *pieces)


def swap_heads(pieces):
    return [pieces[0]] + [
        lax.ppermute(pieces[j], "head", [(h, (h + j) % NH) for h in range(NH)]) for j in range(1, NH)
    ]


def swap_owners(pieces, sign):
    return [pieces[0]] + [
        lax.ppermute(pieces[j], "y", [(h, (h + sign * j) % NY) for h in range(NY)]) for j in range(1, NY)
    ]


def pack_kernel(idx_ref, *refs):
    pieces, outs = refs[:NH], refs[NH:-1]
    block = refs[-1]
    tok = pieces[0].shape[0]

    @pl.when(pl.program_id(0) == 0)
    def _():
        for j in range(NH):
            block[j * tok : (j + 1) * tok, :] = pieces[j][...]

    hot = idx_ref[...] == lax.broadcasted_iota(jnp.int32, (idx_ref.shape[0], block.shape[0]), 1)
    value = dot(hot.astype(F32).astype(BF), block[...], 1, 0).astype(BF)
    for j in range(len(outs)):

        @pl.when(pl.program_id(0) == j)
        def _(j=j):
            outs[j][...] = value


def pack(idx, pieces, count):
    tok, width = pieces[0].shape
    step = idx.shape[0] // count
    whole = pl.BlockSpec((tok, width), lambda i: (0, 0))
    return pl.pallas_call(
        pack_kernel,
        grid=(count,),
        in_specs=[pl.BlockSpec((step, 1), lambda i: (i, 0))] + [whole] * NH,
        out_specs=[pl.BlockSpec((step, width), lambda i: (0, 0))] * count,
        out_shape=[jax.ShapeDtypeStruct((step, width), BF)] * count,
        scratch_shapes=[pltpu.VMEM((tok * NH, width), BF)],
        name="pack_rows",
    )(idx, *pieces)


def unpack_kernel(idx_ref, *refs):
    ins, outs = refs[: len(refs) - NH - 1], refs[len(refs) - NH - 1 : -1]
    block = refs[-1]
    tok = outs[0].shape[0]
    part = ins[0].shape[0]

    @pl.when(pl.program_id(0) == 0)
    def _():
        for k in range(len(ins)):
            block[k * part : (k + 1) * part, :] = ins[k][...]

    row = lax.broadcasted_iota(jnp.int32, (tok, block.shape[0]), 0) + pl.program_id(0) * tok
    hot = (row == idx_ref[...]).astype(F32).astype(BF)
    value = dot(hot, block[...], 1, 0).astype(BF)
    for j in range(NH):

        @pl.when(pl.program_id(0) == j)
        def _(j=j):
            outs[j][...] = value


def unpack(idx, pieces, tok):
    part, width = pieces[0].shape
    return pl.pallas_call(
        unpack_kernel,
        grid=(NH,),
        in_specs=[pl.BlockSpec(idx.shape, lambda i: (0, 0))]
        + [pl.BlockSpec((part, width), lambda i: (0, 0))] * len(pieces),
        out_specs=[pl.BlockSpec((tok, width), lambda i: (0, 0))] * NH,
        out_shape=[jax.ShapeDtypeStruct((tok, width), BF)] * NH,
        scratch_shapes=[pltpu.VMEM((part * len(pieces), width), BF)],
        name="unpack_rows",
    )(idx, *pieces)


def pick(index, count, rows):
    hot = index[:, None] == jnp.arange(count, dtype=jnp.int32)[None, :]
    return dot(hot.astype(BF), rows, 1, 0).astype(BF)


def body(
    queries, keys, values, upstream, send_rows, recv_rows, doc_lengths, pair_docs, response_mask, policy_logp, ref_logp
):
    tok = queries.shape[0]
    rows = tok * NH
    width = queries.shape[1] // NH
    seq = ("z", "y")
    slots = send_rows.shape[1]
    my_y = lax.axis_index("y")
    send = send_rows[0]
    ahead = (my_y + jnp.arange(NY, dtype=jnp.int32)) % NY
    behind = (my_y - jnp.arange(NY, dtype=jnp.int32)) % NY
    send_y = jnp.take(send.reshape(NZ, NY, CAP), ahead, axis=1).transpose(1, 0, 2).reshape(slots)
    recv = recv_rows[0]
    me = lax.axis_index("head")
    me_arr = me.reshape(1).astype(jnp.int32)

    def turned(index, sign):
        piece = (sign * (index // tok - me)) % NH
        return jnp.where(index >= 0, piece * tok + index % tok, -1)

    kv = split(me_arr, [keys, values])
    kv = swap_heads(kv)
    (kv,) = pack(turned(send, -1)[:, None], kv, 1)
    kv = lax.all_to_all(kv.reshape(NZ * NY, CAP, 2 * D), seq, 0, 0).reshape(slots, 2 * D)
    kv = pick(recv, slots, kv)
    kv = lax.all_gather(kv, "z", axis=0)

    place_of = jnp.arange(rows, dtype=jnp.int32)
    slot_id = jnp.arange(slots, dtype=jnp.int32)
    pos = jnp.sum(jnp.where(recv[None, :] == slot_id[:, None], place_of[None, :] + 1, 0), axis=1) - 1
    ends = jnp.cumsum(doc_lengths[0])
    doc_row = jnp.sum((place_of[:, None] >= ends[None, :]).astype(jnp.int32), axis=1)
    member = doc_row[:, None] == jnp.arange(4, dtype=jnp.int32)[None, :]
    gap_row = response_mask.astype(F32) * (policy_logp - ref_logp)
    gap = jnp.sum(jnp.where(member, gap_row[:, None], 0.0), axis=0)
    part = jnp.broadcast_to(pos.astype(F32).reshape(NZ, 1, NY * CAP), (NZ, NY, NY * CAP)).reshape(NZ * NY, NY * CAP)
    small = jnp.broadcast_to(jnp.concatenate([gap, ends.astype(F32), jnp.zeros((56,), F32)])[None, :], (NZ * NY, 64))
    got = lax.all_to_all(jnp.concatenate([part, small], axis=1), seq, 0, 0)
    gaps = got[:, 192:196].reshape(128)
    mine = lax.dynamic_index_in_dim(got.reshape(NZ, NY, 256), my_y, 1, keepdims=False)
    other = pair_docs.reshape(64, 2)[:, ::-1].reshape(128)
    doc_id = jnp.arange(128, dtype=jnp.int32)
    own_hot = pair_docs[:, None] == doc_id[None, :]
    sign = 1.0 - 2.0 * (doc_id % 2).astype(F32)
    own_gap = jnp.sum(jnp.where(own_hot, gaps[None, :], 0.0), axis=1)
    other_gap = jnp.sum(jnp.where(other[:, None] == doc_id[None, :], gaps[None, :], 0.0), axis=1)
    margin = BETA * (own_gap - other_gap) * sign
    weight = -sign * (BETA * jax.nn.sigmoid(-margin))
    doc_coef = jnp.sum(jnp.where(own_hot, weight[:, None], 0.0), axis=0)
    my_coef = lax.dynamic_index_in_dim(doc_coef.reshape(NZ, NY, 4), my_y, 1, keepdims=False)
    q_pos = mine[:, :192].astype(jnp.int32)
    q_ends = mine[:, 196:200].astype(jnp.int32)
    past = q_pos[:, :, None] >= q_ends[:, None, :]
    q_doc = jnp.sum(past.astype(jnp.int32), axis=2)
    q_start = jnp.max(jnp.where(past, q_ends[:, None, :], 0), axis=2)
    in_doc = (q_doc[:, :, None] == jnp.arange(4, dtype=jnp.int32)) & (q_pos[:, :, None] >= 0)
    coef = jnp.sum(jnp.where(in_doc, my_coef[:, None, :], 0.0), axis=2)
    q_pos = jnp.take(q_pos.reshape(NZ, NY, CAP), behind, axis=1)
    q_start = jnp.take(q_start.reshape(NZ, NY, CAP), behind, axis=1)
    coef = jnp.take(coef.reshape(NZ, NY, CAP), behind, axis=1)[:, :, :, None]
    past_last = jnp.max(q_pos, axis=2) + 1
    first = jnp.min(jnp.where(q_pos >= 0, q_start, rows), axis=2)
    first = jnp.clip(jnp.minimum(first, past_last) // 16 * 16, 0, rows - 128)
    blocks = jnp.clip((past_last - first + 127) // 128, 1, 8)
    blocks = jnp.where(blocks > 5, 8, blocks)
    first = jnp.minimum(first, rows - 128 * blocks)
    rng = jnp.stack([first.reshape(-1), blocks.reshape(-1)])
    heads = width // D
    pos_lane = jnp.tile(q_pos, (1, 1, heads))[:, :, None, :]
    start_lane = jnp.tile(q_start, (1, 1, heads))[:, :, None, :]

    in_index = turned(send_y, -1)[:, None]
    out_index = turned(send_y, 1)[None, :]

    def move_in(x):
        x = split(me_arr, [x])
        x = swap_heads(x)
        x = pack(in_index, x, NY)
        x = swap_owners(x, 1)
        return [t.reshape(NZ, CAP, width) for t in x]

    q = move_in(queries)
    u = move_in(upstream)

    gq, gkv = attention(rng, q, u, kv, pos_lane, start_lane, coef)

    gkv = lax.psum_scatter(gkv, "z", scatter_dimension=0)
    gkv = pick(pos, rows, gkv).reshape(NZ * NY, CAP, 2 * D)
    gkv = lax.all_to_all(gkv, seq, 0, 0).reshape(slots, 2 * D)
    gkv = unpack(turned(send, 1)[None, :], [gkv], tok)
    gkv = swap_heads(gkv)
    gk, gv = join(me_arr, gkv, 2)
    gq = swap_owners([t.reshape(NZ * CAP, width) for t in gq], -1)
    gq = unpack(out_index, gq, tok)
    gq = swap_heads(gq)
    (gq,) = join(me_arr, gq, 1)
    return (gq, gk, gv)


def solution(mesh):
    grid = Mesh(mesh.devices.reshape(NZ, NY, NH), ("z", "y", "head"))
    tokens = P(("z", "y", "head"), None)
    group = P(("z", "y"), None)
    line = P(("z", "y"))
    return jax.shard_map(
        body,
        mesh=grid,
        in_specs=(tokens, tokens, tokens, tokens, group, group, group, P(), line, line, line),
        out_specs=(tokens, tokens, tokens),
        check_vma=False,
    )
```

```python
import functools
import math

import jax
import jax.numpy as jnp
from jax import lax
from jax.experimental import pallas as pl
from jax.experimental.pallas import tpu as pltpu
from jax.sharding import Mesh
from jax.sharding import PartitionSpec as P


D = 128
CAP = 48
NZ = 8
NY = 4
NH = 8
BETA = 0.1
BF = jnp.bfloat16
F32 = jnp.float32


def dot(a, b, ca, cb):
    return lax.dot_general(a, b, (((ca,), (cb,)), ((), ())), preferred_element_type=F32)


WINDOWS = (1, 2, 5, 8)


def attention_kernel(rng, *refs):
    q_in, u_in = refs[:NY], refs[NY : 2 * NY]
    kv_ref, p_ref, st_ref, c_ref = refs[2 * NY : 2 * NY + 4]
    gq_out, gkv_ref = refs[2 * NY + 4 : 3 * NY + 4], refs[3 * NY + 4]
    q_scr, u_scr, gq_scr, gk_acc, gv_acc = refs[3 * NY + 5 :]
    owner = pl.program_id(0)
    heads = q_scr.shape[2] // D
    lanes = heads * CAP
    scale = 1.0 / math.sqrt(D)
    gk_acc[...] = jnp.zeros_like(gk_acc)
    gv_acc[...] = jnp.zeros_like(gv_acc)
    for y in range(NY):
        q_scr[y] = q_in[y][0]
        u_scr[y] = u_in[y][0]

    def stack(block):
        return jnp.concatenate([block[:, h * D : (h + 1) * D] for h in range(heads)], axis=0)

    def window(y, base, size):
        q = stack(q_scr[y])
        g = stack((u_scr[y].astype(F32) * c_ref[0, y]).astype(BF))
        pos = p_ref[0, y]
        start = st_ref[0, y]
        keys = kv_ref[0, pl.ds(base, size), :D]
        vals = kv_ref[0, pl.ds(base, size), D:]
        s = dot(keys, q, 1, 1) * scale
        key = lax.broadcasted_iota(jnp.int32, (size, lanes), 0) + base
        s = jnp.where((key >= start) & (key <= pos), s, -1e30)
        e = jnp.exp(s - jnp.max(s, axis=0, keepdims=True))
        dp = dot(vals, g, 1, 1)
        inverse = 1.0 / jnp.sum(e, axis=0, keepdims=True)
        row_dot = jnp.sum(e * dp, axis=0, keepdims=True) * inverse
        probs = e * inverse
        gs = (probs * (dp - row_dot) * scale).astype(BF)
        gv_acc[pl.ds(base, size), :] += dot(probs.astype(BF), g, 1, 0)
        gk_acc[pl.ds(base, size), :] += dot(gs, q, 1, 0)
        gq = dot(keys.T, gs, 1, 0).T.astype(BF)
        for h in range(heads):
            gq_scr[y, :, h * D : (h + 1) * D] = gq[h * CAP : (h + 1) * CAP, :]

    def one(y, carry):
        base = pl.multiple_of(rng[0, owner * NY + y], 16)
        blocks = rng[1, owner * NY + y]
        for n in WINDOWS:
            pl.when(blocks == n)(lambda n=n: window(y, base, n * 128))
        return carry

    lax.fori_loop(0, NY, one, 0)
    for y in range(NY):
        gq_out[y][0] = gq_scr[y]
    gkv_ref[0, :, :D] = gk_acc[...].astype(BF)
    gkv_ref[0, :, D:] = gv_acc[...].astype(BF)


def attention(rng, q, u, kv, pos, start, coef):
    rows = kv.shape[1]
    width = q[0].shape[2]
    lanes = (width // D) * CAP
    slot = pl.BlockSpec((1, CAP, width), lambda i, r: (i, 0, 0))
    pair = pl.BlockSpec((1, rows, 2 * D), lambda i, r: (i, 0, 0))
    lane = pl.BlockSpec((1, NY, 1, lanes), lambda i, r: (i, 0, 0, 0))
    out = pl.pallas_call(
        attention_kernel,
        grid_spec=pltpu.PrefetchScalarGridSpec(
            num_scalar_prefetch=1,
            grid=(NZ,),
            in_specs=[slot] * (2 * NY) + [pair, lane, lane, pl.BlockSpec((1, NY, CAP, 1), lambda i, r: (i, 0, 0, 0))],
            out_specs=[slot] * NY + [pair],
            scratch_shapes=[pltpu.VMEM((NY, CAP, width), BF)] * 3 + [pltpu.VMEM((rows, D), F32)] * 2,
        ),
        out_shape=[jax.ShapeDtypeStruct(q[0].shape, BF)] * NY + [jax.ShapeDtypeStruct(kv.shape, BF)],
        name="owner_attention",
    )(rng, *q, *u, kv, pos, start, coef)
    return out[:NY], out[NY]


def split_kernel(me_ref, *refs):
    count = len(refs) - NH
    ins, outs = refs[:count], refs[count:]
    width = ins[0].shape[1] // NH
    for j in range(NH):
        to = lax.rem(me_ref[0] + j, NH)
        cols = pl.ds(pl.multiple_of(to * width, 128), width)
        for k in range(count):
            outs[j][:, k * width : (k + 1) * width] = ins[k][:, cols]


def split(me, arrays):
    tok = arrays[0].shape[0]
    width = arrays[0].shape[1] // NH * len(arrays)
    return pl.pallas_call(
        split_kernel,
        in_specs=[pl.BlockSpec(memory_space=pltpu.SMEM)] + [pl.BlockSpec(memory_space=pltpu.VMEM)] * len(arrays),
        out_specs=[pl.BlockSpec(memory_space=pltpu.VMEM)] * NH,
        out_shape=[jax.ShapeDtypeStruct((tok, width), BF)] * NH,
        name="split_heads",
    )(me, *arrays)


def join_kernel(me_ref, *refs):
    ins, outs = refs[:NH], refs[NH:]
    width = outs[0].shape[1] // NH
    for j in range(NH):
        src = lax.rem(me_ref[0] + (NH - j), NH)
        cols = pl.ds(pl.multiple_of(src * width, 128), width)
        for k in range(len(outs)):
            outs[k][:, cols] = ins[j][:, k * width : (k + 1) * width]


def join(me, pieces, count):
    tok, width = pieces[0].shape
    return pl.pallas_call(
        join_kernel,
        in_specs=[pl.BlockSpec(memory_space=pltpu.SMEM)] + [pl.BlockSpec(memory_space=pltpu.VMEM)] * NH,
        out_specs=[pl.BlockSpec(memory_space=pltpu.VMEM)] * count,
        out_shape=[jax.ShapeDtypeStruct((tok, width // count * NH), BF)] * count,
        name="join_heads",
    )(me, *pieces)


def split_all_kernel(*refs):
    ins, out = refs[:-1], refs[-1]
    width = ins[0].shape[1] // NH
    for h in range(NH):
        for k in range(len(ins)):
            out[h, :, k * width : (k + 1) * width] = ins[k][:, h * width : (h + 1) * width]


def split_all(arrays):
    tok = arrays[0].shape[0]
    width = arrays[0].shape[1] // NH * len(arrays)
    return pl.pallas_call(
        split_all_kernel, out_shape=jax.ShapeDtypeStruct((NH, tok, width), BF), name="split_all_heads"
    )(*arrays)


def join_all_kernel(in_ref, *outs):
    width = outs[0].shape[1] // NH
    for h in range(NH):
        for k in range(len(outs)):
            outs[k][:, h * width : (h + 1) * width] = in_ref[h, :, k * width : (k + 1) * width]


def join_all(block, count):
    tok, width = block.shape[1:]
    return pl.pallas_call(
        join_all_kernel,
        out_shape=[jax.ShapeDtypeStruct((tok, width // count * NH), BF)] * count,
        name="join_all_heads",
    )(block)


def swap_heads(pieces):
    return [pieces[0]] + [
        lax.ppermute(pieces[j], "head", [(h, (h + j) % NH) for h in range(NH)]) for j in range(1, NH)
    ]


def swap_owners(pieces, sign):
    return [pieces[0]] + [
        lax.ppermute(pieces[j], "y", [(h, (h + sign * j) % NY) for h in range(NY)]) for j in range(1, NY)
    ]


def pack_kernel(idx_ref, *refs):
    block = refs[-1]
    tok = refs[0].shape[0]
    count = block.shape[0] // tok
    pieces, outs = refs[:count], refs[count:-1]

    @pl.when(pl.program_id(0) == 0)
    def _():
        for j in range(count):
            block[j * tok : (j + 1) * tok, :] = pieces[j][...]

    hot = idx_ref[...] == lax.broadcasted_iota(jnp.int32, (idx_ref.shape[0], block.shape[0]), 1)
    value = dot(hot.astype(F32).astype(BF), block[...], 1, 0).astype(BF)
    for j in range(len(outs)):

        @pl.when(pl.program_id(0) == j)
        def _(j=j):
            outs[j][...] = value


def pack(idx, pieces, count):
    tok, width = pieces[0].shape
    step = idx.shape[0] // count
    whole = pl.BlockSpec((tok, width), lambda i: (0, 0))
    return pl.pallas_call(
        pack_kernel,
        grid=(count,),
        in_specs=[pl.BlockSpec((step, 1), lambda i: (i, 0))] + [whole] * len(pieces),
        out_specs=[pl.BlockSpec((step, width), lambda i: (0, 0))] * count,
        out_shape=[jax.ShapeDtypeStruct((step, width), BF)] * count,
        scratch_shapes=[pltpu.VMEM((tok * len(pieces), width), BF)],
        name="pack_rows",
    )(idx, *pieces)


def unpack_kernel(idx_ref, *refs):
    ins, outs = refs[: len(refs) - NH - 1], refs[len(refs) - NH - 1 : -1]
    block = refs[-1]
    tok = outs[0].shape[0]
    part = ins[0].shape[0]

    @pl.when(pl.program_id(0) == 0)
    def _():
        for k in range(len(ins)):
            block[k * part : (k + 1) * part, :] = ins[k][...]

    row = lax.broadcasted_iota(jnp.int32, (tok, block.shape[0]), 0) + pl.program_id(0) * tok
    hot = (row == idx_ref[...]).astype(F32).astype(BF)
    value = dot(hot, block[...], 1, 0).astype(BF)
    for j in range(NH):

        @pl.when(pl.program_id(0) == j)
        def _(j=j):
            outs[j][...] = value


def unpack(idx, pieces, tok):
    part, width = pieces[0].shape
    return pl.pallas_call(
        unpack_kernel,
        grid=(NH,),
        in_specs=[pl.BlockSpec(idx.shape, lambda i: (0, 0))]
        + [pl.BlockSpec((part, width), lambda i: (0, 0))] * len(pieces),
        out_specs=[pl.BlockSpec((tok, width), lambda i: (0, 0))] * NH,
        out_shape=[jax.ShapeDtypeStruct((tok, width), BF)] * NH,
        scratch_shapes=[pltpu.VMEM((part * len(pieces), width), BF)],
        name="unpack_rows",
    )(idx, *pieces)


def pick_kernel(by_row, idx_ref, in_ref, out):
    shape = (out.shape[0], in_ref.shape[0])
    if by_row:
        hot = lax.broadcasted_iota(jnp.int32, shape, 0) + pl.program_id(0) * shape[0] == idx_ref[...]
    else:
        hot = idx_ref[...] == lax.broadcasted_iota(jnp.int32, shape, 1)
    out[...] = dot(hot.astype(F32).astype(BF), in_ref[...], 1, 0).astype(BF)


def pick(idx, rows, step, count=None):
    by_row = count is not None
    total = count if by_row else idx.shape[0]
    idx = idx[None, :] if by_row else idx[:, None]
    idx_spec = pl.BlockSpec(idx.shape, lambda i: (0, 0)) if by_row else pl.BlockSpec((step, 1), lambda i: (i, 0))
    return pl.pallas_call(
        functools.partial(pick_kernel, by_row),
        grid=(total // step,),
        in_specs=[idx_spec, pl.BlockSpec(rows.shape, lambda i: (0, 0))],
        out_specs=pl.BlockSpec((step, rows.shape[1]), lambda i: (i, 0)),
        out_shape=jax.ShapeDtypeStruct((total, rows.shape[1]), BF),
        name="pick_rows",
    )(idx, rows)


def body(
    queries, keys, values, upstream, send_rows, recv_rows, doc_lengths, pair_docs, response_mask, policy_logp, ref_logp
):
    tok = queries.shape[0]
    rows = tok * NH
    width = queries.shape[1] // NH
    seq = ("z", "y")
    slots = send_rows.shape[1]
    my_y = lax.axis_index("y")
    send = send_rows[0]
    ahead = (my_y + jnp.arange(NY, dtype=jnp.int32)) % NY
    behind = (my_y - jnp.arange(NY, dtype=jnp.int32)) % NY
    send_y = jnp.take(send.reshape(NZ, NY, CAP), ahead, axis=1).transpose(1, 0, 2).reshape(slots)
    recv = recv_rows[0]
    me = lax.axis_index("head")
    me_arr = me.reshape(1).astype(jnp.int32)

    def turned(index, sign):
        piece = (sign * (index // tok - me)) % NH
        return jnp.where(index >= 0, piece * tok + index % tok, -1)

    place_of = jnp.arange(rows, dtype=jnp.int32)
    slot_id = jnp.arange(slots, dtype=jnp.int32)
    pos = jnp.sum(jnp.where(recv[None, :] == slot_id[:, None], place_of[None, :] + 1, 0), axis=1) - 1
    ends = jnp.cumsum(doc_lengths[0])
    doc_row = jnp.sum((place_of[:, None] >= ends[None, :]).astype(jnp.int32), axis=1)
    member = doc_row[:, None] == jnp.arange(4, dtype=jnp.int32)[None, :]
    gap_row = response_mask.astype(F32) * (policy_logp - ref_logp)
    gap = jnp.sum(jnp.where(member, gap_row[:, None], 0.0), axis=0)
    part = jnp.broadcast_to(pos.astype(F32).reshape(NZ, 1, NY * CAP), (NZ, NY, NY * CAP)).reshape(NZ * NY, NY * CAP)
    small = jnp.concatenate([gap, ends.astype(F32), jnp.zeros((56,), F32)])
    note = jnp.concatenate([part, jnp.broadcast_to(small[None, :], (NZ * NY, 64))], axis=1)
    got = lax.all_to_all(note, seq, 0, 0)

    kv = split_all([keys, values])
    kv = lax.all_to_all(kv, "head", 0, 0).reshape(rows, 2 * D)
    kv = pick(send, kv, slots // 4)
    kv = lax.all_to_all(kv.reshape(NZ * NY, CAP, 2 * D), seq, 0, 0).reshape(slots, 2 * D)
    kv = pick(recv, kv, rows // 4)
    kv = lax.all_gather(kv, "z", axis=0)

    gaps = got[:, 192:196].reshape(128)
    mine = lax.dynamic_index_in_dim(got.reshape(NZ, NY, 256), my_y, 1, keepdims=False)
    other = pair_docs.reshape(64, 2)[:, ::-1].reshape(128)
    doc_id = jnp.arange(128, dtype=jnp.int32)
    own_hot = pair_docs[:, None] == doc_id[None, :]
    sign = 1.0 - 2.0 * (doc_id % 2).astype(F32)
    own_gap = jnp.sum(jnp.where(own_hot, gaps[None, :], 0.0), axis=1)
    other_gap = jnp.sum(jnp.where(other[:, None] == doc_id[None, :], gaps[None, :], 0.0), axis=1)
    margin = BETA * (own_gap - other_gap) * sign
    weight = -sign * (BETA * jax.nn.sigmoid(-margin))
    doc_coef = jnp.sum(jnp.where(own_hot, weight[:, None], 0.0), axis=0)
    my_coef = lax.dynamic_index_in_dim(doc_coef.reshape(NZ, NY, 4), my_y, 1, keepdims=False)
    q_pos = mine[:, :192].astype(jnp.int32)
    q_ends = mine[:, 196:200].astype(jnp.int32)
    past = q_pos[:, :, None] >= q_ends[:, None, :]
    q_doc = jnp.sum(past.astype(jnp.int32), axis=2)
    q_start = jnp.max(jnp.where(past, q_ends[:, None, :], 0), axis=2)
    in_doc = (q_doc[:, :, None] == jnp.arange(4, dtype=jnp.int32)) & (q_pos[:, :, None] >= 0)
    coef = jnp.sum(jnp.where(in_doc, my_coef[:, None, :], 0.0), axis=2)
    q_pos = jnp.take(q_pos.reshape(NZ, NY, CAP), behind, axis=1)
    q_start = jnp.take(q_start.reshape(NZ, NY, CAP), behind, axis=1)
    coef = jnp.take(coef.reshape(NZ, NY, CAP), behind, axis=1)[:, :, :, None]
    past_last = jnp.max(q_pos, axis=2) + 1
    first = jnp.min(jnp.where(q_pos >= 0, q_start, rows), axis=2)
    first = jnp.clip(jnp.minimum(first, past_last) // 16 * 16, 0, rows - 128)
    blocks = jnp.clip((past_last - first + 127) // 128, 1, 8)
    blocks = jnp.where(blocks > 5, 8, jnp.where(blocks > 2, 5, blocks))
    first = jnp.minimum(first, rows - 128 * blocks)
    rng = jnp.stack([first.reshape(-1), blocks.reshape(-1)])
    heads = width // D
    pos_lane = jnp.tile(q_pos, (1, 1, heads))[:, :, None, :]
    start_lane = jnp.tile(q_start, (1, 1, heads))[:, :, None, :]

    out_index = turned(send_y, 1)[None, :]

    def to_owners(x):
        x = swap_owners(x, 1)
        return [t.reshape(NZ, CAP, width) for t in x]

    q = split(me_arr, [queries])
    q = swap_heads(q)
    q = pack(turned(send_y, -1)[:, None], q, NY)
    q = to_owners(q)
    u = split_all([upstream])
    u = lax.all_to_all(u, "head", 0, 0).reshape(rows, width)
    u = pack(send_y[:, None], [u], NY)
    u = to_owners(u)

    gq, gkv = attention(rng, q, u, kv, pos_lane, start_lane, coef)

    gkv = lax.psum_scatter(gkv, "z", scatter_dimension=0)
    gkv = pick(pos, gkv, slots // 4).reshape(NZ * NY, CAP, 2 * D)
    gkv = lax.all_to_all(gkv, seq, 0, 0).reshape(slots, 2 * D)
    gkv = pick(send, gkv, rows // 4, rows).reshape(NH, tok, 2 * D)
    gkv = lax.all_to_all(gkv, "head", 0, 0)
    gk, gv = join_all(gkv, 2)
    gq = swap_owners([t.reshape(NZ * CAP, width) for t in gq], -1)
    gq = unpack(out_index, gq, tok)
    gq = swap_heads(gq)
    (gq,) = join(me_arr, gq, 1)
    return (gq, gk, gv)


def solution(mesh):
    grid = Mesh(mesh.devices.reshape(NZ, NY, NH), ("z", "y", "head"))
    tokens = P(("z", "y", "head"), None)
    group = P(("z", "y"), None)
    line = P(("z", "y"))
    return jax.shard_map(
        body,
        mesh=grid,
        in_specs=(tokens, tokens, tokens, tokens, group, group, group, P(), line, line, line),
        out_specs=(tokens, tokens, tokens),
        check_vma=False,
    )
```

```python
import functools
import math

import jax
import jax.numpy as jnp
from jax import lax
from jax.experimental import pallas as pl
from jax.experimental.pallas import tpu as pltpu
from jax.sharding import Mesh
from jax.sharding import PartitionSpec as P


D = 128
CAP = 48
NZ = 8
NY = 4
NH = 8
BETA = 0.1
BF = jnp.bfloat16
F32 = jnp.float32


def dot(a, b, ca, cb):
    return lax.dot_general(a, b, (((ca,), (cb,)), ((), ())), preferred_element_type=F32)


WINDOWS = (1, 2, 3, 4, 5, 8)


def attention_kernel(rng, *refs):
    q_in, u_in = refs[:NY], refs[NY : 2 * NY]
    kv_ref, p_ref, st_ref, c_ref = refs[2 * NY : 2 * NY + 4]
    gq_out, gkv_ref = refs[2 * NY + 4 : 3 * NY + 4], refs[3 * NY + 4]
    q_scr, u_scr, gq_scr, gk_acc, gv_acc = refs[3 * NY + 5 :]
    owner = pl.program_id(0)
    heads = q_scr.shape[2] // D
    lanes = heads * CAP
    scale = 1.0 / math.sqrt(D)
    gk_acc[...] = jnp.zeros_like(gk_acc)
    gv_acc[...] = jnp.zeros_like(gv_acc)
    for y in range(NY):
        q_scr[y] = q_in[y][0]
        u_scr[y] = u_in[y][0]

    def stack(block):
        return jnp.concatenate([block[:, h * D : (h + 1) * D] for h in range(heads)], axis=0)

    def window(y, base, size):
        q = stack(q_scr[y])
        g = stack((u_scr[y].astype(F32) * c_ref[0, y]).astype(BF))
        pos = p_ref[0, y]
        start = st_ref[0, y]
        keys = kv_ref[0, pl.ds(base, size), :D]
        vals = kv_ref[0, pl.ds(base, size), D:]
        s = dot(keys, q, 1, 1) * scale
        key = lax.broadcasted_iota(jnp.int32, (size, lanes), 0) + base
        s = jnp.where((key >= start) & (key <= pos), s, -1e30)
        e = jnp.exp(s - jnp.max(s, axis=0, keepdims=True))
        dp = dot(vals, g, 1, 1)
        inverse = 1.0 / jnp.sum(e, axis=0, keepdims=True)
        row_dot = jnp.sum(e * dp, axis=0, keepdims=True) * inverse
        probs = e * inverse
        gs = (probs * (dp - row_dot) * scale).astype(BF)
        gv_acc[pl.ds(base, size), :] += dot(probs.astype(BF), g, 1, 0)
        gk_acc[pl.ds(base, size), :] += dot(gs, q, 1, 0)
        gq = dot(keys.T, gs, 1, 0).T.astype(BF)
        for h in range(heads):
            gq_scr[y, :, h * D : (h + 1) * D] = gq[h * CAP : (h + 1) * CAP, :]

    def one(y, carry):
        base = pl.multiple_of(rng[0, owner * NY + y], 16)
        blocks = rng[1, owner * NY + y]
        for n in WINDOWS:
            pl.when(blocks == n)(lambda n=n: window(y, base, n * 128))
        return carry

    lax.fori_loop(0, NY, one, 0)
    for y in range(NY):
        gq_out[y][0] = gq_scr[y]
    gkv_ref[0, :, :D] = gk_acc[...].astype(BF)
    gkv_ref[0, :, D:] = gv_acc[...].astype(BF)


def attention(rng, q, u, kv, pos, start, coef):
    rows = kv.shape[1]
    width = q[0].shape[2]
    lanes = (width // D) * CAP
    slot = pl.BlockSpec((1, CAP, width), lambda i, r: (i, 0, 0))
    pair = pl.BlockSpec((1, rows, 2 * D), lambda i, r: (i, 0, 0))
    lane = pl.BlockSpec((1, NY, 1, lanes), lambda i, r: (i, 0, 0, 0))
    out = pl.pallas_call(
        attention_kernel,
        grid_spec=pltpu.PrefetchScalarGridSpec(
            num_scalar_prefetch=1,
            grid=(NZ,),
            in_specs=[slot] * (2 * NY) + [pair, lane, lane, pl.BlockSpec((1, NY, CAP, 1), lambda i, r: (i, 0, 0, 0))],
            out_specs=[slot] * NY + [pair],
            scratch_shapes=[pltpu.VMEM((NY, CAP, width), BF)] * 3 + [pltpu.VMEM((rows, D), F32)] * 2,
        ),
        out_shape=[jax.ShapeDtypeStruct(q[0].shape, BF)] * NY + [jax.ShapeDtypeStruct(kv.shape, BF)],
        name="owner_attention",
    )(rng, *q, *u, kv, pos, start, coef)
    return out[:NY], out[NY]


def split_kernel(me_ref, *refs):
    count = len(refs) - NH
    ins, outs = refs[:count], refs[count:]
    width = ins[0].shape[1] // NH
    for j in range(NH):
        to = lax.rem(me_ref[0] + j, NH)
        cols = pl.ds(pl.multiple_of(to * width, 128), width)
        for k in range(count):
            outs[j][:, k * width : (k + 1) * width] = ins[k][:, cols]


def split(me, arrays):
    tok = arrays[0].shape[0]
    width = arrays[0].shape[1] // NH * len(arrays)
    return pl.pallas_call(
        split_kernel,
        in_specs=[pl.BlockSpec(memory_space=pltpu.SMEM)] + [pl.BlockSpec(memory_space=pltpu.VMEM)] * len(arrays),
        out_specs=[pl.BlockSpec(memory_space=pltpu.VMEM)] * NH,
        out_shape=[jax.ShapeDtypeStruct((tok, width), BF)] * NH,
        name="split_heads",
    )(me, *arrays)


def join_kernel(me_ref, *refs):
    ins, outs = refs[:NH], refs[NH:]
    width = outs[0].shape[1] // NH
    for j in range(NH):
        src = lax.rem(me_ref[0] + (NH - j), NH)
        cols = pl.ds(pl.multiple_of(src * width, 128), width)
        for k in range(len(outs)):
            outs[k][:, cols] = ins[j][:, k * width : (k + 1) * width]


def join(me, pieces, count):
    tok, width = pieces[0].shape
    return pl.pallas_call(
        join_kernel,
        in_specs=[pl.BlockSpec(memory_space=pltpu.SMEM)] + [pl.BlockSpec(memory_space=pltpu.VMEM)] * NH,
        out_specs=[pl.BlockSpec(memory_space=pltpu.VMEM)] * count,
        out_shape=[jax.ShapeDtypeStruct((tok, width // count * NH), BF)] * count,
        name="join_heads",
    )(me, *pieces)


def split_all_kernel(*refs):
    ins, out = refs[:-1], refs[-1]
    width = ins[0].shape[1] // NH
    for h in range(NH):
        for k in range(len(ins)):
            out[h, :, k * width : (k + 1) * width] = ins[k][:, h * width : (h + 1) * width]


def split_all(arrays):
    tok = arrays[0].shape[0]
    width = arrays[0].shape[1] // NH * len(arrays)
    return pl.pallas_call(
        split_all_kernel, out_shape=jax.ShapeDtypeStruct((NH, tok, width), BF), name="split_all_heads"
    )(*arrays)


def join_all_kernel(in_ref, *outs):
    width = outs[0].shape[1] // NH
    for h in range(NH):
        for k in range(len(outs)):
            outs[k][:, h * width : (h + 1) * width] = in_ref[h, :, k * width : (k + 1) * width]


def join_all(block, count):
    tok, width = block.shape[1:]
    return pl.pallas_call(
        join_all_kernel,
        out_shape=[jax.ShapeDtypeStruct((tok, width // count * NH), BF)] * count,
        name="join_all_heads",
    )(block)


def swap_heads(pieces):
    return [pieces[0]] + [
        lax.ppermute(pieces[j], "head", [(h, (h + j) % NH) for h in range(NH)]) for j in range(1, NH)
    ]


def swap_owners(pieces, sign):
    return [pieces[0]] + [
        lax.ppermute(pieces[j], "y", [(h, (h + sign * j) % NY) for h in range(NY)]) for j in range(1, NY)
    ]


def pack_kernel(count, idx_ref, *refs):
    pieces, outs = refs[:-count], refs[-count:]
    block = jnp.concatenate([p[...] for p in pieces], axis=0)
    hot = idx_ref[...] == lax.broadcasted_iota(jnp.int32, (idx_ref.shape[0], block.shape[0]), 1)
    value = dot(hot.astype(F32).astype(BF), block, 1, 0).astype(BF)
    for j in range(count):

        @pl.when(pl.program_id(0) == j)
        def _(j=j):
            outs[j][...] = value


def pack(idx, pieces, count):
    tok, width = pieces[0].shape
    step = idx.shape[0] // count
    whole = pl.BlockSpec((tok, width), lambda i: (0, 0))
    return pl.pallas_call(
        functools.partial(pack_kernel, count),
        grid=(count,),
        in_specs=[pl.BlockSpec((step, 1), lambda i: (i, 0))] + [whole] * len(pieces),
        out_specs=[pl.BlockSpec((step, width), lambda i: (0, 0))] * count,
        out_shape=[jax.ShapeDtypeStruct((step, width), BF)] * count,
        name="pack_rows",
    )(idx, *pieces)


def unpack_kernel(idx_ref, *refs):
    ins, outs = refs[:-NH], refs[-NH:]
    tok = outs[0].shape[0]
    block = jnp.concatenate([p[...] for p in ins], axis=0)
    row = lax.broadcasted_iota(jnp.int32, (2 * tok, block.shape[0]), 0) + pl.program_id(0) * (2 * tok)
    hot = (row == idx_ref[...]).astype(F32).astype(BF)
    value = dot(hot, block, 1, 0).astype(BF)
    for j in range(NH):

        @pl.when(pl.program_id(0) == j // 2)
        def _(j=j):
            outs[j][...] = value[j % 2 * tok : (j % 2 + 1) * tok, :]


def unpack(idx, pieces, tok):
    part, width = pieces[0].shape
    return pl.pallas_call(
        unpack_kernel,
        grid=(NH // 2,),
        in_specs=[pl.BlockSpec(idx.shape, lambda i: (0, 0))]
        + [pl.BlockSpec((part, width), lambda i: (0, 0))] * len(pieces),
        out_specs=[pl.BlockSpec((tok, width), lambda i: (0, 0))] * NH,
        out_shape=[jax.ShapeDtypeStruct((tok, width), BF)] * NH,
        name="unpack_rows",
    )(idx, *pieces)


def pick_kernel(by_row, idx_ref, in_ref, out):
    shape = (out.shape[0], in_ref.shape[0])
    if by_row:
        hot = lax.broadcasted_iota(jnp.int32, shape, 0) + pl.program_id(0) * shape[0] == idx_ref[...]
    else:
        hot = idx_ref[...] == lax.broadcasted_iota(jnp.int32, shape, 1)
    out[...] = dot(hot.astype(F32).astype(BF), in_ref[...], 1, 0).astype(BF)


def pick(idx, rows, step, count=None):
    by_row = count is not None
    total = count if by_row else idx.shape[0]
    idx = idx[None, :] if by_row else idx[:, None]
    idx_spec = pl.BlockSpec(idx.shape, lambda i: (0, 0)) if by_row else pl.BlockSpec((step, 1), lambda i: (i, 0))
    return pl.pallas_call(
        functools.partial(pick_kernel, by_row),
        grid=(total // step,),
        in_specs=[idx_spec, pl.BlockSpec(rows.shape, lambda i: (0, 0))],
        out_specs=pl.BlockSpec((step, rows.shape[1]), lambda i: (i, 0)),
        out_shape=jax.ShapeDtypeStruct((total, rows.shape[1]), BF),
        name="pick_rows",
    )(idx, rows)


def body(
    queries, keys, values, upstream, send_rows, recv_rows, doc_lengths, pair_docs, response_mask, policy_logp, ref_logp
):
    tok = queries.shape[0]
    rows = tok * NH
    width = queries.shape[1] // NH
    seq = ("z", "y")
    slots = send_rows.shape[1]
    my_y = lax.axis_index("y")
    send = send_rows[0]
    ahead = (my_y + jnp.arange(NY, dtype=jnp.int32)) % NY
    behind = (my_y - jnp.arange(NY, dtype=jnp.int32)) % NY
    send_y = jnp.take(send.reshape(NZ, NY, CAP), ahead, axis=1).transpose(1, 0, 2).reshape(slots)
    recv = recv_rows[0]
    me = lax.axis_index("head")
    me_arr = me.reshape(1).astype(jnp.int32)

    def turned(index, sign):
        piece = (sign * (index // tok - me)) % NH
        return jnp.where(index >= 0, piece * tok + index % tok, -1)

    place_of = jnp.arange(rows, dtype=jnp.int32)
    slot_id = jnp.arange(slots, dtype=jnp.int32)
    pos = jnp.sum(jnp.where(recv[None, :] == slot_id[:, None], place_of[None, :] + 1, 0), axis=1) - 1
    ends = jnp.cumsum(doc_lengths[0])
    doc_row = jnp.sum((place_of[:, None] >= ends[None, :]).astype(jnp.int32), axis=1)
    member = doc_row[:, None] == jnp.arange(4, dtype=jnp.int32)[None, :]
    gap_row = response_mask.astype(F32) * (policy_logp - ref_logp)
    gap = jnp.sum(jnp.where(member, gap_row[:, None], 0.0), axis=0)
    part = jnp.broadcast_to(pos.astype(F32).reshape(NZ, 1, NY * CAP), (NZ, NY, NY * CAP)).reshape(NZ * NY, NY * CAP)
    small = jnp.concatenate([gap, ends.astype(F32), jnp.zeros((56,), F32)])
    note = jnp.concatenate([part, jnp.broadcast_to(small[None, :], (NZ * NY, 64))], axis=1)
    got = lax.all_to_all(note, seq, 0, 0)

    kv = split_all([keys, values])
    kv = lax.all_to_all(kv, "head", 0, 0).reshape(rows, 2 * D)
    kv = pick(send, kv, slots // 4)
    kv = lax.all_to_all(kv.reshape(NZ * NY, CAP, 2 * D), seq, 0, 0).reshape(slots, 2 * D)
    kv = pick(recv, kv, rows // 4)
    kv = lax.all_gather(kv, "z", axis=0)

    gaps = got[:, 192:196].reshape(128)
    mine = lax.dynamic_index_in_dim(got.reshape(NZ, NY, 256), my_y, 1, keepdims=False)
    other = pair_docs.reshape(64, 2)[:, ::-1].reshape(128)
    doc_id = jnp.arange(128, dtype=jnp.int32)
    own_hot = pair_docs[:, None] == doc_id[None, :]
    sign = 1.0 - 2.0 * (doc_id % 2).astype(F32)
    own_gap = jnp.sum(jnp.where(own_hot, gaps[None, :], 0.0), axis=1)
    other_gap = jnp.sum(jnp.where(other[:, None] == doc_id[None, :], gaps[None, :], 0.0), axis=1)
    margin = BETA * (own_gap - other_gap) * sign
    weight = -sign * (BETA * jax.nn.sigmoid(-margin))
    doc_coef = jnp.sum(jnp.where(own_hot, weight[:, None], 0.0), axis=0)
    my_coef = lax.dynamic_index_in_dim(doc_coef.reshape(NZ, NY, 4), my_y, 1, keepdims=False)
    q_pos = mine[:, :192].astype(jnp.int32)
    q_ends = mine[:, 196:200].astype(jnp.int32)
    past = q_pos[:, :, None] >= q_ends[:, None, :]
    q_doc = jnp.sum(past.astype(jnp.int32), axis=2)
    q_start = jnp.max(jnp.where(past, q_ends[:, None, :], 0), axis=2)
    in_doc = (q_doc[:, :, None] == jnp.arange(4, dtype=jnp.int32)) & (q_pos[:, :, None] >= 0)
    coef = jnp.sum(jnp.where(in_doc, my_coef[:, None, :], 0.0), axis=2)
    q_pos = jnp.take(q_pos.reshape(NZ, NY, CAP), behind, axis=1)
    q_start = jnp.take(q_start.reshape(NZ, NY, CAP), behind, axis=1)
    coef = jnp.take(coef.reshape(NZ, NY, CAP), behind, axis=1)[:, :, :, None]
    past_last = jnp.max(q_pos, axis=2) + 1
    first = jnp.min(jnp.where(q_pos >= 0, q_start, rows), axis=2)
    first = jnp.clip(jnp.minimum(first, past_last) // 16 * 16, 0, rows - 128)
    blocks = jnp.clip((past_last - first + 127) // 128, 1, 8)
    blocks = jnp.where(blocks > 5, 8, blocks)
    first = jnp.minimum(first, rows - 128 * blocks)
    rng = jnp.stack([first.reshape(-1), blocks.reshape(-1)])
    heads = width // D
    pos_lane = jnp.tile(q_pos, (1, 1, heads))[:, :, None, :]
    start_lane = jnp.tile(q_start, (1, 1, heads))[:, :, None, :]

    out_index = turned(send_y, 1)[None, :]

    def to_owners(x):
        x = swap_owners(x, 1)
        return [t.reshape(NZ, CAP, width) for t in x]

    q = split(me_arr, [queries])
    q = swap_heads(q)
    q = pack(turned(send_y, -1)[:, None], q, NY)
    q = to_owners(q)
    u = split_all([upstream])
    u = lax.all_to_all(u, "head", 0, 0).reshape(rows, width)
    u = pack(send_y[:, None], [u], NY)
    u = to_owners(u)

    gq, gkv = attention(rng, q, u, kv, pos_lane, start_lane, coef)

    gkv = lax.psum_scatter(gkv, "z", scatter_dimension=0)
    gkv = pick(pos, gkv, slots // 4).reshape(NZ * NY, CAP, 2 * D)
    gkv = lax.all_to_all(gkv, seq, 0, 0).reshape(slots, 2 * D)
    gkv = pick(send, gkv, rows // 4, rows).reshape(NH, tok, 2 * D)
    gkv = lax.all_to_all(gkv, "head", 0, 0)
    gk, gv = join_all(gkv, 2)
    gq = swap_owners([t.reshape(NZ * CAP, width) for t in gq], -1)
    gq = unpack(out_index, gq, tok)
    gq = swap_heads(gq)
    (gq,) = join(me_arr, gq, 1)
    return (gq, gk, gv)


def solution(mesh):
    grid = Mesh(mesh.devices.reshape(NZ, NY, NH), ("z", "y", "head"))
    tokens = P(("z", "y", "head"), None)
    group = P(("z", "y"), None)
    line = P(("z", "y"))
    return jax.shard_map(
        body,
        mesh=grid,
        in_specs=(tokens, tokens, tokens, tokens, group, group, group, P(), line, line, line),
        out_specs=(tokens, tokens, tokens),
        check_vma=False,
    )
```
